32 devices in a mesh: cls: 4 (over y, x), row: 8 (over z, core).
Axes of the slice: x: 2, y: 2, z: 4, core: 2. Of those that a mesh axis runs over, the one named last changes fastest.
Arguments:
- codes: int32 [2048, 1024], P('row'), may hold values from 0 to 63
- split_feature: int32 [16, 7], P('cls'), may hold values from 0 to 1023
- split_bin: int32 [16, 7], P('cls'), may hold values from 0 to 62
- labels: int32 [2048], P('row'), may hold values from 0 to 15
- margins: float32 [2048, 16], P('row', 'cls'), may hold values from -11 to 11
Outputs:
- best_gain: float32 [16, 4], P('cls')
- leaf_value: float32 [16, 8], P('cls')
- grad_next: float32 [2048, 16], P('row', 'cls')
- hess_next: float32 [2048, 16], P('row', 'cls')
The draws below stay inside these ranges and needn't reach their ends.
All inputs are finite; a program needn't handle non-finite values.
Results may differ from the reference program's by a relative error of at most 0.0013.
Values may be sent and summed in bfloat16 or wider, within the bound.
A program may use at most 64 MiB of HBM per device.

```python
import math
import jax
import jax.numpy as jnp
from jax import lax

F = 1024
BINS = 64
LEVEL = 2
ROWS = 2048
CLASSES = 16
NODES = 4
NTOT = 7


def draw_margins(key, part):
    noise_key = jax.random.fold_in(key, 11)
    offset_key = jax.random.fold_in(key, 23)
    ramp = 1.0 + 2.0 * jnp.arange(ROWS, dtype=jnp.float32) / ROWS
    noise = jnp.clip(jax.random.normal(noise_key, (ROWS, CLASSES), jnp.float32), -4.0, 4.0)
    offset = jax.random.uniform(offset_key, (CLASSES,), jnp.float32, -2.0, 2.0)
    return noise + offset[None, :] * ramp[:, None]


def with_ends(drawn, rng, low, high):
    longest = drawn.shape.index(max(drawn.shape))
    spots = []
    for shift in (0, 1):
        where = [jax.random.randint(jax.random.fold_in(rng, axis), (), 0, length) for axis, length in enumerate(drawn.shape)]
        where[longest] = (where[longest] + shift) % drawn.shape[longest]
        spots.append(tuple(where))
    return drawn.at[spots[0]].set(low).at[spots[1]].set(high)


def setup_inputs(seed: int = 0) -> dict:
    arg_keys = jax.random.split(jax.random.key(seed), 6)
    return {
        "codes": with_ends(jax.random.randint(arg_keys[0], (ROWS, F), 0, BINS), jax.random.fold_in(arg_keys[0], 1), 0, BINS - 1).astype(jnp.int32),
        "split_feature": with_ends(jax.random.randint(arg_keys[1], (CLASSES, NTOT), 0, F), jax.random.fold_in(arg_keys[1], 1), 0, F - 1).astype(jnp.int32),
        "split_bin": with_ends(jax.random.randint(arg_keys[2], (CLASSES, NTOT), 0, BINS - 1), jax.random.fold_in(arg_keys[2], 1), 0, (BINS - 1) - 1).astype(jnp.int32),
        "labels": with_ends(jax.random.randint(arg_keys[3], (ROWS,), 0, CLASSES), jax.random.fold_in(arg_keys[3], 1), 0, CLASSES - 1).astype(jnp.int32),
        "margins": draw_margins(jax.random.fold_in(arg_keys[5], 71), 0),
    }


reg_weight = 1.0
shrink_rate = 0.3


def class_stats(margins, labels):
    expon = jnp.exp(margins)
    totals = jnp.sum(expon, axis=1, keepdims=True)
    probab = expon / totals
    target = (labels[:, None] == jnp.arange(CLASSES, dtype=jnp.int32)[None, :]).astype(jnp.float32)
    return probab - target, 2.0 * probab * (1.0 - probab)


def lookup(table, node_index):
    return jnp.take_along_axis(table.T, node_index, axis=0)


def reference(codes, split_feature, split_bin, labels, margins):
    grad, hess = class_stats(margins, labels)
    grad_low = grad.astype(jnp.bfloat16)
    hess_low = hess.astype(jnp.bfloat16)
    node_index = jnp.zeros((ROWS, CLASSES), jnp.int32)
    for level in range(LEVEL):
        feature = lookup(split_feature, node_index)
        code_here = jnp.take_along_axis(codes, feature, axis=1)
        node_index = jnp.where(code_here <= lookup(split_bin, node_index), 2 * node_index + 1, 2 * node_index + 2)
    local_node = node_index - (NODES - 1)
    member = (local_node[:, :, None] == jnp.arange(NODES, dtype=jnp.int32)[None, None, :]).astype(jnp.float32)
    stacked = jnp.stack([grad_low.astype(jnp.float32), hess_low.astype(jnp.float32)])
    weights_rows = (stacked[:, :, :, None] * member[None]).transpose(0, 2, 3, 1).reshape(2 * CLASSES * NODES, ROWS)
    block = math.gcd(F, 16)

    def feature_block(index):
        sub_codes = lax.dynamic_slice_in_dim(codes, index * block, block, 1)
        onehot = (sub_codes[:, :, None] == jnp.arange(BINS, dtype=jnp.int32)[None, None, :]).astype(jnp.float32)
        onehot = onehot.reshape(ROWS, block * BINS)
        return jnp.dot(weights_rows, onehot, precision=lax.Precision.HIGHEST, preferred_element_type=jnp.float32)

    blocks = lax.map(feature_block, jnp.arange(F // block, dtype=jnp.int32))
    hist = blocks.reshape(F // block, 2, CLASSES, NODES, block, BINS).transpose(1, 2, 3, 0, 4, 5)
    hist = hist.reshape(2, CLASSES, NODES, F, BINS)
    cumul = jnp.cumsum(hist, axis=-1)
    g_left = cumul[0, :, :, :, :-1]
    h_left = cumul[1, :, :, :, :-1]
    g_all = cumul[0, :, :, :, -1:]
    h_all = cumul[1, :, :, :, -1:]
    gain = g_left * g_left / (h_left + reg_weight) + (g_all - g_left) ** 2 / (h_all - h_left + reg_weight) - g_all * g_all / (h_all + reg_weight)
    best_gain = jnp.max(gain / (h_all + reg_weight), axis=(2, 3))
    leaf_feat = split_feature[:, NODES - 1:]
    leaf_bin = split_bin[:, NODES - 1:]
    chosen = jnp.take_along_axis(hist, leaf_feat[None, :, :, None, None], axis=3)[:, :, :, 0, :]
    below = (jnp.arange(BINS, dtype=jnp.int32)[None, None, :] <= leaf_bin[:, :, None]).astype(jnp.float32)
    left_sum = jnp.sum(chosen * below[None], axis=-1)
    right_sum = jnp.sum(chosen * (1.0 - below[None]), axis=-1)
    left_value = -shrink_rate * left_sum[0] / (left_sum[1] + reg_weight)
    right_value = -shrink_rate * right_sum[0] / (right_sum[1] + reg_weight)
    leaf_value = jnp.stack([left_value, right_value], axis=-1).reshape(CLASSES, 2 * NODES)
    final_feat = lookup(split_feature, node_index)
    code_last = jnp.take_along_axis(codes, final_feat, axis=1)
    side = (code_last > lookup(split_bin, node_index)).astype(jnp.int32)
    leaf_index = 2 * local_node + side
    update = jnp.take_along_axis(leaf_value.T, leaf_index, axis=0)
    grad_next, hess_next = class_stats(margins + update, labels)
    return best_gain, leaf_value, grad_next, hess_next
```

```python
import functools
import jax
import jax.numpy as jnp
from jax import lax
from jax.experimental import pallas as pl
from jax.experimental.pallas import tpu as pltpu
from jax.sharding import PartitionSpec as P

BINS = 64
REG = 1.0
SHRINK = 0.3
MESH = pl.DeviceIdType.MESH


def kernel(dims, codes_ref, sf_ref, sb_ref, lab_ref, mar_ref, bg_ref, lv_ref, gn_ref, hn_ref,
           sel, picked, csend, crecv, blocks, marg, tags, codef, wts, le, nextg, nexth,
           gsend, grecv, hsend, hrecv,
           row_s, row_r, cls_s, cls_r, cod_s, cod_r, g_s, g_r, h_s, h_r):
    nc, nr, C, Rl, F, NT, chunk = dims
    CT, R = C * nc, Rl * nr
    nodes = (NT + 1) // 2
    leaves = 2 * nodes
    levels = nodes.bit_length() - 1
    fq = F // nc
    fb = fq // nr
    f32, bf16 = jnp.float32, jnp.bfloat16
    c = lax.axis_index("cls")
    r = lax.axis_index("row")

    def row_peer(k):
        return (c, lax.rem(r + k, nr))

    def cls_peer(k):
        return (lax.rem(c + k, nc), r)

    barrier = pltpu.get_barrier_semaphore()
    for k in range(1, nr):
        pl.semaphore_signal(barrier, inc=1, device_id=row_peer(k), device_id_type=MESH)
    for k in range(1, nc):
        pl.semaphore_signal(barrier, inc=1, device_id=cls_peer(k), device_id_type=MESH)

    lane = lax.broadcasted_iota(jnp.int32, (C, F), 1)
    sel[...] = jnp.zeros_like(sel)
    for n in range(NT):
        sel[n * C:(n + 1) * C, :] = jnp.where(lane == sf_ref[:, n:n + 1], 1.0, 0.0).astype(f32)
    low = codes_ref[...].astype(f32).astype(bf16)
    picked[...] = lax.dot_general(sel[...].astype(bf16), low, (((1,), (1,)), ((), ())),
                                  preferred_element_type=f32)
    bins = sb_ref[...].astype(f32)
    at = jnp.zeros((C, Rl), jnp.int32)
    for level in range(levels + 1):
        first = 2 ** level - 1
        code = picked[first * C:(first + 1) * C, :]
        cut = jnp.broadcast_to(bins[:, first:first + 1], (C, Rl))
        for j in range(1, 2 ** level):
            n = first + j
            hit = at == j
            code = jnp.where(hit, picked[n * C:(n + 1) * C, :], code)
            cut = jnp.where(hit, bins[:, n:n + 1], cut)
        at = 2 * at + jnp.where(code > cut, 1, 0)
    ids = c * C + lax.broadcasted_iota(jnp.int32, (C, Rl), 0)
    tag = at.astype(f32) + jnp.where(lab_ref[...] == ids, float(leaves), 0.0)
    blocks[c, r, 0:C, :] = mar_ref[...]
    blocks[c, r, C:2 * C, :] = tag

    pl.semaphore_wait(barrier, nr - 1 + nc - 1)

    def row_copy(k):
        return pltpu.make_async_remote_copy(
            src_ref=blocks.at[c, r], dst_ref=blocks.at[c, r], send_sem=row_s.at[k],
            recv_sem=row_r.at[k], device_id=row_peer(k), device_id_type=MESH)

    def cls_copy(k):
        return pltpu.make_async_remote_copy(
            src_ref=blocks.at[c], dst_ref=blocks.at[c], send_sem=cls_s.at[k],
            recv_sem=cls_r.at[k], device_id=cls_peer(k), device_id_type=MESH)

    def cod_copy(k):
        return pltpu.make_async_remote_copy(
            src_ref=csend.at[lax.rem(r + k, nr)], dst_ref=crecv.at[r], send_sem=cod_s.at[k],
            recv_sem=cod_r.at[k], device_id=row_peer(k), device_id_type=MESH)

    rows = [row_copy(k) for k in range(1, nr)]
    for d in rows:
        d.start()

    quarter = codes_ref[:, pl.ds(pl.multiple_of(c * fq, 128), fq)].astype(f32)
    turned = quarter.T.astype(bf16)
    for j in range(nr):
        csend[j] = turned[j * fb:(j + 1) * fb, :]
    cods = [cod_copy(k) for k in range(1, nr)]
    for d in cods:
        d.start()
    crecv[r] = csend[r]

    for d in rows:
        d.wait_recv()
    clss = [cls_copy(k) for k in range(1, nc)]
    for d in clss:
        d.start()
    for d in clss:
        d.wait_recv()

    for a in range(nc):
        for q in range(nr):
            marg[a * C:(a + 1) * C, q * Rl:(q + 1) * Rl] = blocks[a, q, 0:C, :]
            tags[a * C:(a + 1) * C, q * Rl:(q + 1) * Rl] = blocks[a, q, C:2 * C, :]

    expon = jnp.exp(marg[...])
    tag_all = tags[...]
    target = jnp.where(tag_all >= leaves, 1.0, 0.0).astype(f32)
    leaf = tag_all - leaves * target
    probab = expon / jnp.sum(expon, axis=0, keepdims=True)
    grad = (probab - target).astype(bf16).astype(f32)
    hess = (2.0 * probab * (1.0 - probab)).astype(bf16).astype(f32)
    g_leaf, h_leaf = [], []
    for n in range(nodes):
        gn_, hn_ = [], []
        for s in range(2):
            hit = leaf == float(2 * n + s)
            gs = jnp.where(hit, grad, 0.0)
            hs = jnp.where(hit, hess, 0.0)
            gn_.append(gs)
            hn_.append(hs)
            g_leaf.append(jnp.sum(gs, axis=1, keepdims=True))
            h_leaf.append(jnp.sum(hs, axis=1, keepdims=True))
        wts[n * CT:(n + 1) * CT, :] = (gn_[0] + gn_[1]).astype(bf16)
        wts[(nodes + n) * CT:(nodes + n + 1) * CT, :] = (hn_[0] + hn_[1]).astype(bf16)
    values = [-SHRINK * g / (h + REG) for g, h in zip(g_leaf, h_leaf)]
    g_all = [g_leaf[2 * n] + g_leaf[2 * n + 1] for n in range(nodes)]
    h_all = [h_leaf[2 * n] + h_leaf[2 * n + 1] for n in range(nodes)]

    for d in cods:
        d.wait_recv()
    for q in range(nr):
        codef[:, q * Rl:(q + 1) * Rl] = crecv[q].astype(f32)
    above = (lax.broadcasted_iota(jnp.int32, (BINS, R), 0) + 1).astype(f32).astype(bf16)
    zero, one = jnp.zeros((), bf16), jnp.ones((), bf16)
    width = chunk * BINS
    last = lax.rem(lax.broadcasted_iota(jnp.int32, (CT, width), 1), BINS) == BINS - 1
    best = [None] * nodes
    for i in range(fb // chunk):
        for j in range(chunk):
            row = jnp.broadcast_to(codef[i * chunk + j:i * chunk + j + 1, :], (BINS, R)).astype(bf16)
            le[i % 2, j * BINS:(j + 1) * BINS, :] = jnp.clip(above - row, zero, one)
        sums = lax.dot_general(wts[...], le[i % 2], (((1,), (1,)), ((), ())),
                               preferred_element_type=f32)
        for n in range(nodes):
            gl = sums[n * CT:(n + 1) * CT, :]
            hl = sums[(nodes + n) * CT:(nodes + n + 1) * CT, :]
            gr = g_all[n] - gl
            hr = h_all[n] - hl + REG
            hl = hl + REG
            gain = (gl * gl * hr + gr * gr * hl) / (hl * hr)
            gain = jnp.where(last, -jnp.inf, gain)
            best[n] = gain if best[n] is None else jnp.maximum(best[n], gain)

    spot = lax.broadcasted_iota(jnp.int32, (CT, 128), 1)
    tops = jnp.zeros((CT, 128), f32)
    for n in range(nodes):
        top = jnp.max(best[n], axis=1, keepdims=True)
        den = h_all[n] + REG
        top = (top - g_all[n] * g_all[n] / den) / den
        tops = jnp.where(spot == n, top, tops)
    for a in range(nc):
        gsend[a] = tops[a * C:(a + 1) * C, :]

    def g_copy(k):
        return pltpu.make_async_remote_copy(
            src_ref=gsend.at[lax.rem(c + k, nc)], dst_ref=grecv.at[k], send_sem=g_s.at[k],
            recv_sem=g_r.at[k], device_id=cls_peer(k), device_id_type=MESH)

    def h_copy(k):
        return pltpu.make_async_remote_copy(
            src_ref=hsend, dst_ref=hrecv.at[k], send_sem=h_s.at[k],
            recv_sem=h_r.at[k], device_id=row_peer(k), device_id_type=MESH)

    gs_ = [g_copy(k) for k in range(1, nc)]
    for d in gs_:
        d.start()

    here = pl.ds(pl.multiple_of(r * Rl, 128), Rl)
    tag_own = tags[:, here]
    target_own = jnp.where(tag_own >= leaves, 1.0, 0.0).astype(f32)
    leaf_own = tag_own - leaves * target_own
    update = jnp.zeros((CT, Rl), f32)
    for l in range(leaves):
        update = jnp.where(leaf_own == float(l), values[l], update)
    expon2 = jnp.exp(marg[:, here] + update)
    prob2 = expon2 / jnp.sum(expon2, axis=0, keepdims=True)
    gnext = prob2 - target_own
    hnext = 2.0 * prob2 * (1.0 - prob2)
    spot2 = lax.broadcasted_iota(jnp.int32, (CT, 128), 1)
    val = jnp.zeros((CT, 128), f32)
    for l in range(leaves):
        val = jnp.where(spot2 == l, values[l], val)
    for a in range(nc):
        nextg[a, :, 0:Rl] = gnext[a * C:(a + 1) * C, :]
        nextg[a, :, Rl:Rl + 128] = val[a * C:(a + 1) * C, :]
        nexth[a] = hnext[a * C:(a + 1) * C, :]
    gn_ref[...] = nextg[c, :, 0:Rl]
    hn_ref[...] = nexth[c]
    lv_ref[...] = nextg[c, :, Rl:Rl + leaves]

    top = gsend[c]
    for k in range(1, nc):
        gs_[k - 1].wait_recv()
        top = jnp.maximum(top, grecv[k])
    hsend[...] = top
    hs_ = [h_copy(k) for k in range(1, nr)]
    for d in hs_:
        d.start()
    for k in range(1, nr):
        hs_[k - 1].wait_recv()
        top = jnp.maximum(top, hrecv[k])
    bg_ref[...] = top[:, 0:nodes]
    for d in rows + clss + cods + gs_ + hs_:
        d.wait_send()


def local(codes, split_feature, split_bin, labels, margins):
    Rl, F = codes.shape
    C, NT = split_feature.shape
    nc, nr = lax.axis_size("cls"), lax.axis_size("row")
    nodes = (NT + 1) // 2
    CT, R = C * nc, Rl * nr
    fb = F // (nc * nr)
    chunk = min(4, fb)
    f32, bf16 = jnp.float32, jnp.bfloat16
    pad = -(-NT * C // 16) * 16
    dma = pltpu.SemaphoreType.DMA
    vmem = pl.BlockSpec(memory_space=pltpu.VMEM)
    best, leaf, grad, hess = pl.pallas_call(
        functools.partial(kernel, (nc, nr, C, Rl, F, NT, chunk)),
        out_shape=(jax.ShapeDtypeStruct((C, nodes), f32), jax.ShapeDtypeStruct((C, 2 * nodes), f32),
                   jax.ShapeDtypeStruct((C, Rl), f32), jax.ShapeDtypeStruct((C, Rl), f32)),
        in_specs=[vmem] * 5,
        out_specs=(vmem,) * 4,
        scratch_shapes=[
            pltpu.VMEM((pad, F), f32), pltpu.VMEM((pad, Rl), f32),
            pltpu.VMEM((nr, fb, Rl), bf16), pltpu.VMEM((nr, fb, Rl), bf16),
            pltpu.VMEM((nc, nr, 2 * C, Rl), f32),
            pltpu.VMEM((CT, R), f32), pltpu.VMEM((CT, R), f32),
            pltpu.VMEM((fb, R), f32), pltpu.VMEM((2 * nodes * CT, R), bf16),
            pltpu.VMEM((2, chunk * BINS, R), bf16),
            pltpu.VMEM((nc, C, Rl + 128), f32), pltpu.VMEM((nc, C, Rl), f32),
            pltpu.VMEM((nc, C, 128), f32), pltpu.VMEM((nc, C, 128), f32),
            pltpu.VMEM((C, 128), f32), pltpu.VMEM((nr, C, 128), f32),
            dma((nr,)), dma((nr,)), dma((nc,)), dma((nc,)), dma((nr,)), dma((nr,)),
            dma((nc,)), dma((nc,)), dma((nr,)), dma((nr,)),
        ],
        compiler_params=pltpu.CompilerParams(
            collective_id=0, has_side_effects=True, vmem_limit_bytes=48 * 2 ** 20),
        name="boost",
    )(codes, split_feature, split_bin, labels.reshape(1, Rl), margins.T)
    return best, leaf, grad.T, hess.T


def solution(mesh):
    in_specs = (P("row", None), P("cls", None), P("cls", None), P("row"), P("row", "cls"))
    out_specs = (P("cls", None), P("cls", None), P("row", "cls"), P("row", "cls"))
    return jax.shard_map(local, mesh=mesh, in_specs=in_specs, out_specs=out_specs, check_vma=False)
```

```python
import functools
import jax
import jax.numpy as jnp
from jax import lax
from jax.experimental import pallas as pl
from jax.experimental.pallas import tpu as pltpu
from jax.sharding import PartitionSpec as P

BINS = 64
REG = 1.0
SHRINK = 0.3
MESH = pl.DeviceIdType.MESH


def kernel(dims, codes_in, sf_in, sb_in, lab_in, mar_in, bg_ref, lv_ref, gn_ref, hn_ref,
           codes_ref, sf_ref, sb_ref, lab_ref, mar_ref, sel, picked, csend, crecv, blocks, marg, tags, wts, le, nextg, nexth,
           gsend, grecv,
           in_s, row_s, row_r, cls_s, cls_r, cod_s, cod_r, g_s, g_r):
    nc, nr, C, Rl, F, NT, chunk = dims
    CT, R = C * nc, Rl * nr
    nodes = (NT + 1) // 2
    leaves = 2 * nodes
    levels = nodes.bit_length() - 1
    fq = F // nc
    fb = fq // nr
    f32, bf16 = jnp.float32, jnp.bfloat16
    c = lax.axis_index("cls")
    r = lax.axis_index("row")

    def row_peer(k):
        return (c, lax.rem(r + k, nr))

    def cls_peer(k):
        return (lax.rem(c + k, nc), r)

    def far_peer(kc, kr):
        return (lax.rem(c + kc, nc), lax.rem(r + kr, nr))

    loads = [pltpu.make_async_copy(src, dst, in_s.at[i]) for i, (src, dst) in enumerate(
        [(sf_in, sf_ref), (codes_in, codes_ref), (sb_in, sb_ref), (lab_in, lab_ref), (mar_in, mar_ref)])]
    for d in loads:
        d.start()
    barrier = pltpu.get_barrier_semaphore()
    far = [(kc, kr) for kc in range(nc) for kr in range(nr) if kc + kr > 0]
    for kc, kr in far:
        pl.semaphore_signal(barrier, inc=1, device_id=far_peer(kc, kr), device_id_type=MESH)
    for d in loads:
        d.wait()

    lane = lax.broadcasted_iota(jnp.int32, (C, F), 1)
    sel[...] = jnp.zeros_like(sel)
    for n in range(NT):
        sel[n * C:(n + 1) * C, :] = jnp.where(lane == sf_ref[:, n:n + 1], 1.0, 0.0).astype(f32)
    low = codes_ref[...].astype(f32).astype(bf16)
    picked[...] = lax.dot_general(sel[...].astype(bf16), low, (((1,), (1,)), ((), ())),
                                  preferred_element_type=f32)
    bins = sb_ref[...].astype(f32)
    at = jnp.zeros((C, Rl), jnp.int32)
    for level in range(levels + 1):
        first = 2 ** level - 1
        code = picked[first * C:(first + 1) * C, :]
        cut = jnp.broadcast_to(bins[:, first:first + 1], (C, Rl))
        for j in range(1, 2 ** level):
            n = first + j
            hit = at == j
            code = jnp.where(hit, picked[n * C:(n + 1) * C, :], code)
            cut = jnp.where(hit, bins[:, n:n + 1], cut)
        at = 2 * at + jnp.where(code > cut, 1, 0)
    ids = c * C + lax.broadcasted_iota(jnp.int32, (C, Rl), 0)
    tag = at.astype(f32) + jnp.where(lab_ref[...] == ids, float(leaves), 0.0)
    blocks[c, r, 0:C, :] = mar_ref[...]
    blocks[c, r, C:2 * C, :] = tag

    pl.semaphore_wait(barrier, nc * nr - 1)

    def row_copy(k):
        return pltpu.make_async_remote_copy(
            src_ref=blocks.at[c, r], dst_ref=blocks.at[c, r], send_sem=row_s.at[k],
            recv_sem=row_r.at[k], device_id=row_peer(k), device_id_type=MESH)

    def cls_copy(k, q, slot):
        return pltpu.make_async_remote_copy(
            src_ref=blocks.at[c, q], dst_ref=blocks.at[c, q], send_sem=cls_s.at[k, slot],
            recv_sem=cls_r.at[k, slot], device_id=cls_peer(k), device_id_type=MESH)

    def cod_copy(k):
        return pltpu.make_async_remote_copy(
            src_ref=csend.at[lax.rem(r + k, nr)], dst_ref=crecv.at[r], send_sem=cod_s.at[k],
            recv_sem=cod_r.at[k], device_id=row_peer(k), device_id_type=MESH)

    near = sorted(range(1, nr), key=lambda k: min(k, nr - k))
    rows = {k: row_copy(k) for k in near}
    for d in rows.values():
        d.start()
    clss = [cls_copy(k, r, 0) for k in range(1, nc)]
    for d in clss:
        d.start()

    quarter = codes_ref[:, pl.ds(pl.multiple_of(c * fq, 128), fq)].astype(f32)
    turned = quarter.T.astype(bf16)
    for j in range(nr):
        csend[j] = turned[j * fb:(j + 1) * fb, :]
    cods = {k: cod_copy(k) for k in near}
    for d in cods.values():
        d.start()
    crecv[r] = csend[r]

    for k in near:
        rows[k].wait_recv()
        for m in range(1, nc):
            d = cls_copy(m, lax.rem(r - k + nr, nr), k)
            d.start()
            clss.append(d)

    group = 16
    steps = [(lax.broadcasted_iota(jnp.int32, (group, Rl), 0) + (g * group + 1)).astype(f32).astype(bf16)
             for g in range(BINS // group)]
    zero, one = jnp.zeros((), bf16), jnp.ones((), bf16)
    for k in [0] + near:
        if k:
            cods[k].wait_recv()
        q = lax.rem(r - k + nr, nr)
        there = pl.ds(pl.multiple_of(q * Rl, 128), Rl)
        block = crecv[q].astype(f32)
        for f in range(fb):
            row = jnp.broadcast_to(block[f:f + 1, :], (group, Rl)).astype(bf16)
            for g in range(BINS // group):
                base = f * BINS + g * group
                le[base:base + group, there] = jnp.clip(steps[g] - row, zero, one)
    for d in clss:
        d.wait_recv()

    for a in range(nc):
        for q in range(nr):
            marg[a * C:(a + 1) * C, q * Rl:(q + 1) * Rl] = blocks[a, q, 0:C, :]
            tags[a * C:(a + 1) * C, q * Rl:(q + 1) * Rl] = blocks[a, q, C:2 * C, :]

    expon = jnp.exp(marg[...])
    tag_all = tags[...]
    target = jnp.where(tag_all >= leaves, 1.0, 0.0).astype(f32)
    leaf = tag_all - leaves * target
    probab = expon / jnp.sum(expon, axis=0, keepdims=True)
    grad = (probab - target).astype(bf16).astype(f32)
    hess = (2.0 * probab * (1.0 - probab)).astype(bf16).astype(f32)
    g_leaf, h_leaf = [], []
    for n in range(nodes):
        gn_, hn_ = [], []
        for s in range(2):
            hit = leaf == float(2 * n + s)
            gs = jnp.where(hit, grad, 0.0)
            hs = jnp.where(hit, hess, 0.0)
            gn_.append(gs)
            hn_.append(hs)
            g_leaf.append(jnp.sum(gs, axis=1, keepdims=True))
            h_leaf.append(jnp.sum(hs, axis=1, keepdims=True))
        wts[n * CT:(n + 1) * CT, :] = (gn_[0] + gn_[1]).astype(bf16)
        wts[(nodes + n) * CT:(nodes + n + 1) * CT, :] = (hn_[0] + hn_[1]).astype(bf16)
    values = [-SHRINK * g / (h + REG) for g, h in zip(g_leaf, h_leaf)]
    g_all = [g_leaf[2 * n] + g_leaf[2 * n + 1] for n in range(nodes)]
    h_all = [h_leaf[2 * n] + h_leaf[2 * n + 1] for n in range(nodes)]

    width = chunk * BINS
    last = lax.rem(lax.broadcasted_iota(jnp.int32, (CT, width), 1), BINS) == BINS - 1
    best = [None] * nodes
    for i in range(fb // chunk):
        sums = lax.dot_general(wts[...], le[i * width:(i + 1) * width, :], (((1,), (1,)), ((), ())),
                               preferred_element_type=f32)
        for n in range(nodes):
            gl = sums[n * CT:(n + 1) * CT, :]
            hl = sums[(nodes + n) * CT:(nodes + n + 1) * CT, :]
            gr = g_all[n] - gl
            hr = h_all[n] - hl + REG
            hl = hl + REG
            gain = (gl * gl * hr + gr * gr * hl) / (hl * hr)
            gain = jnp.where(last, -jnp.inf, gain)
            best[n] = gain if best[n] is None else jnp.maximum(best[n], gain)

    spot = lax.broadcasted_iota(jnp.int32, (CT, 128), 1)
    place = lax.rem(lax.broadcasted_iota(jnp.int32, (CT, 128), 0), C) * nodes
    tops = jnp.zeros((CT, 128), f32)
    for n in range(nodes):
        top = jnp.max(best[n], axis=1, keepdims=True)
        den = h_all[n] + REG
        top = (top - g_all[n] * g_all[n] / den) / den
        tops = jnp.where(spot == place + n, top, tops)
    for a in range(nc):
        gsend[a] = jnp.sum(tops[a * C:(a + 1) * C, :], axis=0, keepdims=True)

    def g_copy(kc, kr):
        slot = kc * nr + kr
        return pltpu.make_async_remote_copy(
            src_ref=gsend.at[lax.rem(c + kc, nc)], dst_ref=grecv.at[slot], send_sem=g_s.at[slot],
            recv_sem=g_r.at[slot], device_id=far_peer(kc, kr), device_id_type=MESH)

    gs_ = [g_copy(kc, kr) for kc, kr in far]
    for d in gs_:
        d.start()
    grecv[0] = gsend[c]

    here = pl.ds(pl.multiple_of(r * Rl, 128), Rl)
    tag_own = tags[:, here]
    target_own = jnp.where(tag_own >= leaves, 1.0, 0.0).astype(f32)
    leaf_own = tag_own - leaves * target_own
    update = jnp.zeros((CT, Rl), f32)
    for l in range(leaves):
        update = jnp.where(leaf_own == float(l), values[l], update)
    expon2 = jnp.exp(marg[:, here] + update)
    prob2 = expon2 / jnp.sum(expon2, axis=0, keepdims=True)
    gnext = prob2 - target_own
    hnext = 2.0 * prob2 * (1.0 - prob2)
    spot2 = lax.broadcasted_iota(jnp.int32, (CT, 128), 1)
    val = jnp.zeros((CT, 128), f32)
    for l in range(leaves):
        val = jnp.where(spot2 == l, values[l], val)
    for a in range(nc):
        nextg[a, :, 0:Rl] = gnext[a * C:(a + 1) * C, :]
        nextg[a, :, Rl:Rl + 128] = val[a * C:(a + 1) * C, :]
        nexth[a] = hnext[a * C:(a + 1) * C, :]
    gn_ref[...] = nextg[c, :, 0:Rl]
    hn_ref[...] = nexth[c]
    lv_ref[...] = nextg[c, :, Rl:Rl + leaves]

    for d in list(rows.values()) + clss + list(cods.values()):
        d.wait_send()
    for d in gs_:
        d.wait_recv()
    top = jnp.max(grecv[...], axis=0)
    for i in range(C):
        line = pltpu.roll(top, (128 - i * nodes) % 128, 1) if i else top
        bg_ref[i:i + 1, :] = line[:, 0:nodes]
    for d in gs_:
        d.wait_send()


def put(a, b, c, d, oa, ob, oc, od, sems):
    copies = [pltpu.make_async_copy(x, y, sems.at[i])
              for i, (x, y) in enumerate([(a, oa), (b, ob), (c, oc), (d, od)])]
    for x in copies:
        x.start()
    for x in copies:
        x.wait()


def local(codes, split_feature, split_bin, labels, margins):
    Rl, F = codes.shape
    C, NT = split_feature.shape
    nc, nr = lax.axis_size("cls"), lax.axis_size("row")
    nodes = (NT + 1) // 2
    CT, R = C * nc, Rl * nr
    fb = F // (nc * nr)
    chunk = min(4, fb)
    f32, bf16 = jnp.float32, jnp.bfloat16
    pad = -(-NT * C // 16) * 16
    dma = pltpu.SemaphoreType.DMA
    vmem = pl.BlockSpec(memory_space=pltpu.VMEM)
    hbm = pl.BlockSpec(memory_space=pltpu.HBM)
    any_ = pl.BlockSpec(memory_space=pl.ANY)
    shapes = (jax.ShapeDtypeStruct((C, nodes), f32), jax.ShapeDtypeStruct((C, 2 * nodes), f32),
              jax.ShapeDtypeStruct((C, Rl), f32), jax.ShapeDtypeStruct((C, Rl), f32))
    made = pl.pallas_call(
        functools.partial(kernel, (nc, nr, C, Rl, F, NT, chunk)),
        out_shape=shapes,
        in_specs=[hbm] * 5,
        out_specs=(vmem,) * 4,
        scratch_shapes=[
            pltpu.VMEM((Rl, F), jnp.int32), pltpu.VMEM((C, NT), jnp.int32), pltpu.VMEM((C, NT), jnp.int32),
            pltpu.VMEM((1, Rl), jnp.int32), pltpu.VMEM((C, Rl), f32),
            pltpu.VMEM((pad, F), f32), pltpu.VMEM((pad, Rl), f32),
            pltpu.VMEM((nr, fb, Rl), bf16), pltpu.VMEM((nr, fb, Rl), bf16),
            pltpu.VMEM((nc, nr, 2 * C, Rl), f32),
            pltpu.VMEM((CT, R), f32), pltpu.VMEM((CT, R), f32),
            pltpu.VMEM((2 * nodes * CT, R), bf16),
            pltpu.VMEM((fb * BINS, R), bf16),
            pltpu.VMEM((nc, C, Rl + 128), f32), pltpu.VMEM((nc, C, Rl), f32),
            pltpu.VMEM((nc, 1, 128), f32), pltpu.VMEM((nc * nr, 1, 128), f32),
            dma((5,)), dma((nr,)), dma((nr,)), dma((nc, nr)), dma((nc, nr)), dma((nr,)), dma((nr,)),
            dma((nc * nr,)), dma((nc * nr,)),
        ],
        compiler_params=pltpu.CompilerParams(
            collective_id=0, has_side_effects=True, vmem_limit_bytes=63 * 2 ** 20),
        name="boost",
    )(codes, split_feature, split_bin, labels.reshape(1, Rl), margins.T)
    best, leaf, grad, hess = pl.pallas_call(
        put, out_shape=shapes, in_specs=[any_] * 4, out_specs=(any_,) * 4,
        scratch_shapes=[dma((4,))], name="put",
    )(*made)
    return best, leaf, grad.T, hess.T


def solution(mesh):
    in_specs = (P("row", None), P("cls", None), P("cls", None), P("row"), P("row", "cls"))
    out_specs = (P("cls", None), P("cls", None), P("row", "cls"), P("row", "cls"))
    return jax.shard_map(local, mesh=mesh, in_specs=in_specs, out_specs=out_specs, check_vma=False)
```

```python
import functools
import jax
import jax.numpy as jnp
from jax import lax
from jax.experimental import pallas as pl
from jax.experimental.pallas import tpu as pltpu
from jax.sharding import PartitionSpec as P

BINS = 64
REG = 1.0
SHRINK = 0.3
MESH = pl.DeviceIdType.MESH


def kernel(dims, codes_in, sf_in, sb_in, lab_in, mar_in, bg_ref, lv_ref, gn_ref, hn_ref,
           codes_ref, sf_ref, sb_ref, lab_ref, mar_ref, sel, picked, csend, crecv, blocks, marg, tags, wts, le, nextg, nexth,
           gsend, grecv,
           in_s, row_s, row_r, cls_s, cls_r, cod_s, cod_r, g_s, g_r):
    nc, nr, C, Rl, F, NT, chunk = dims
    CT, R = C * nc, Rl * nr
    nodes = (NT + 1) // 2
    leaves = 2 * nodes
    levels = nodes.bit_length() - 1
    fq = F // nc
    fb = fq // nr
    f32, bf16 = jnp.float32, jnp.bfloat16
    c = lax.axis_index("cls")
    r = lax.axis_index("row")

    cls_at = [jnp.where(c + k >= nc, c + k - nc, c + k) for k in range(nc)]
    row_at = [jnp.where(r + k >= nr, r + k - nr, r + k) for k in range(nr)]

    def row_peer(k):
        return (c, row_at[k])

    def cls_peer(k):
        return (cls_at[k], r)

    def far_peer(kc, kr):
        return (cls_at[kc], row_at[kr])

    loads = [pltpu.make_async_copy(src, dst, in_s.at[i]) for i, (src, dst) in enumerate(
        [(sf_in, sf_ref), (codes_in, codes_ref), (sb_in, sb_ref), (lab_in, lab_ref), (mar_in, mar_ref)])]
    for d in loads:
        d.start()
    barrier = pltpu.get_barrier_semaphore()
    far = [(kc, kr) for kc in range(nc) for kr in range(nr) if kc + kr > 0]
    for k in range(1, nr):
        pl.semaphore_signal(barrier, inc=1, device_id=row_peer(k), device_id_type=MESH)
    for k in range(1, nc):
        pl.semaphore_signal(barrier, inc=1, device_id=cls_peer(k), device_id_type=MESH)
    for d in loads:
        d.wait()

    lane = lax.broadcasted_iota(jnp.int32, (C, F), 1)
    sel[...] = jnp.zeros_like(sel)
    for n in range(NT):
        sel[n * C:(n + 1) * C, :] = jnp.where(lane == sf_ref[:, n:n + 1], 1.0, 0.0).astype(f32)
    low = codes_ref[...].astype(f32).astype(bf16)
    picked[...] = lax.dot_general(sel[...].astype(bf16), low, (((1,), (1,)), ((), ())),
                                  preferred_element_type=f32)
    bins = sb_ref[...].astype(f32)
    at = jnp.zeros((C, Rl), jnp.int32)
    for level in range(levels + 1):
        first = 2 ** level - 1
        code = picked[first * C:(first + 1) * C, :]
        cut = jnp.broadcast_to(bins[:, first:first + 1], (C, Rl))
        for j in range(1, 2 ** level):
            n = first + j
            hit = at == j
            code = jnp.where(hit, picked[n * C:(n + 1) * C, :], code)
            cut = jnp.where(hit, bins[:, n:n + 1], cut)
        at = 2 * at + jnp.where(code > cut, 1, 0)
    ids = c * C + lax.broadcasted_iota(jnp.int32, (C, Rl), 0)
    tag = at.astype(f32) + jnp.where(lab_ref[...] == ids, float(leaves), 0.0)
    blocks[c, r, 0:C, :] = mar_ref[...]
    blocks[c, r, C:2 * C, :] = tag

    pl.semaphore_wait(barrier, nr - 1 + nc - 1)

    def row_copy(k):
        return pltpu.make_async_remote_copy(
            src_ref=blocks.at[c, r], dst_ref=blocks.at[c, r], send_sem=row_s.at[k],
            recv_sem=row_r.at[k], device_id=row_peer(k), device_id_type=MESH)

    def cls_copy(k, q):
        return pltpu.make_async_remote_copy(
            src_ref=blocks.at[c, q], dst_ref=blocks.at[c, q], send_sem=cls_s,
            recv_sem=cls_r, device_id=cls_peer(k), device_id_type=MESH)

    def cod_copy(k):
        return pltpu.make_async_remote_copy(
            src_ref=csend.at[row_at[k]], dst_ref=crecv.at[r], send_sem=cod_s.at[k],
            recv_sem=cod_r.at[k], device_id=row_peer(k), device_id_type=MESH)

    near = sorted(range(1, nr), key=lambda k: min(k, nr - k))
    rows = {k: row_copy(k) for k in near}
    for d in rows.values():
        d.start()
    for k in range(1, nc):
        cls_copy(k, r).start()

    quarter = codes_ref[:, pl.ds(pl.multiple_of(c * fq, 128), fq)].astype(f32)
    turned = quarter.T.astype(bf16)
    for j in range(nr):
        csend[j] = turned[j * fb:(j + 1) * fb, :]
    cods = {k: cod_copy(k) for k in near}
    for d in cods.values():
        d.start()
    crecv[r] = csend[r]

    for k in near:
        rows[k].wait_recv()
        for m in range(1, nc):
            cls_copy(m, row_at[(nr - k) % nr]).start()

    group = 16
    steps = [(lax.broadcasted_iota(jnp.int32, (group, Rl), 0) + (g * group + 1)).astype(f32).astype(bf16)
             for g in range(BINS // group)]
    zero, one = jnp.zeros((), bf16), jnp.ones((), bf16)
    for k in [0] + near:
        if k:
            cods[k].wait_recv()
        q = row_at[(nr - k) % nr]
        there = pl.ds(pl.multiple_of(q * Rl, 128), Rl)
        block = crecv[q].astype(f32)
        for f in range(fb):
            row = jnp.broadcast_to(block[f:f + 1, :], (group, Rl)).astype(bf16)
            for g in range(BINS // group):
                base = f * BINS + g * group
                le[base:base + group, there] = jnp.clip(steps[g] - row, zero, one)
    others = blocks.at[pl.ds(0, nc - 1)]
    gathered = pltpu.make_async_remote_copy(
        src_ref=others, dst_ref=others, send_sem=cls_s, recv_sem=cls_r,
        device_id=cls_peer(1), device_id_type=MESH)
    gathered.wait_recv()

    for a in range(nc):
        for q in range(nr):
            marg[a * C:(a + 1) * C, q * Rl:(q + 1) * Rl] = blocks[a, q, 0:C, :]
            tags[a * C:(a + 1) * C, q * Rl:(q + 1) * Rl] = blocks[a, q, C:2 * C, :]

    expon = jnp.exp(marg[...])
    tag_all = tags[...]
    target = jnp.where(tag_all >= leaves, 1.0, 0.0).astype(f32)
    leaf = tag_all - leaves * target
    probab = expon / jnp.sum(expon, axis=0, keepdims=True)
    grad = (probab - target).astype(bf16).astype(f32)
    hess = (2.0 * probab * (1.0 - probab)).astype(bf16).astype(f32)
    g_leaf, h_leaf = [], []
    for n in range(nodes):
        gn_, hn_ = [], []
        for s in range(2):
            hit = leaf == float(2 * n + s)
            gs = jnp.where(hit, grad, 0.0)
            hs = jnp.where(hit, hess, 0.0)
            gn_.append(gs)
            hn_.append(hs)
            g_leaf.append(jnp.sum(gs, axis=1, keepdims=True))
            h_leaf.append(jnp.sum(hs, axis=1, keepdims=True))
        wts[n * CT:(n + 1) * CT, :] = (gn_[0] + gn_[1]).astype(bf16)
        wts[(nodes + n) * CT:(nodes + n + 1) * CT, :] = (hn_[0] + hn_[1]).astype(bf16)
    values = [-SHRINK * g / (h + REG) for g, h in zip(g_leaf, h_leaf)]
    g_all = [g_leaf[2 * n] + g_leaf[2 * n + 1] for n in range(nodes)]
    h_all = [h_leaf[2 * n] + h_leaf[2 * n + 1] for n in range(nodes)]

    width = chunk * BINS
    last = lax.rem(lax.broadcasted_iota(jnp.int32, (CT, width), 1), BINS) == BINS - 1
    best = [None] * nodes
    for i in range(fb // chunk):
        sums = lax.dot_general(wts[...], le[i * width:(i + 1) * width, :], (((1,), (1,)), ((), ())),
                               preferred_element_type=f32)
        for n in range(nodes):
            gl = sums[n * CT:(n + 1) * CT, :]
            hl = sums[(nodes + n) * CT:(nodes + n + 1) * CT, :]
            gr = g_all[n] - gl
            hr = h_all[n] - hl + REG
            hl = hl + REG
            gain = (gl * gl * hr + gr * gr * hl) / (hl * hr)
            gain = jnp.where(last, -jnp.inf, gain)
            best[n] = gain if best[n] is None else jnp.maximum(best[n], gain)

    spot = lax.broadcasted_iota(jnp.int32, (CT, 128), 1)
    place = lax.rem(lax.broadcasted_iota(jnp.int32, (CT, 128), 0), C) * nodes
    tops = jnp.zeros((CT, 128), f32)
    for n in range(nodes):
        top = jnp.max(best[n], axis=1, keepdims=True)
        den = h_all[n] + REG
        top = (top - g_all[n] * g_all[n] / den) / den
        tops = jnp.where(spot == place + n, top, tops)
    for a in range(nc):
        gsend[a] = jnp.sum(tops[a * C:(a + 1) * C, :], axis=0, keepdims=True)

    def g_copy(kc, kr):
        slot = kc * nr + kr
        return pltpu.make_async_remote_copy(
            src_ref=gsend.at[cls_at[kc]], dst_ref=grecv.at[slot], send_sem=g_s,
            recv_sem=g_r, device_id=far_peer(kc, kr), device_id_type=MESH)

    gs_ = [g_copy(kc, kr) for kc, kr in far]
    for d in gs_:
        d.start()
    grecv[0] = gsend[c]

    here = pl.ds(pl.multiple_of(r * Rl, 128), Rl)
    tag_own = tags[:, here]
    target_own = jnp.where(tag_own >= leaves, 1.0, 0.0).astype(f32)
    leaf_own = tag_own - leaves * target_own
    update = jnp.zeros((CT, Rl), f32)
    for l in range(leaves):
        update = jnp.where(leaf_own == float(l), values[l], update)
    expon2 = jnp.exp(marg[:, here] + update)
    prob2 = expon2 / jnp.sum(expon2, axis=0, keepdims=True)
    gnext = prob2 - target_own
    hnext = 2.0 * prob2 * (1.0 - prob2)
    spot2 = lax.broadcasted_iota(jnp.int32, (CT, 128), 1)
    val = jnp.zeros((CT, 128), f32)
    for l in range(leaves):
        val = jnp.where(spot2 == l, values[l], val)
    for a in range(nc):
        nextg[a, :, 0:Rl] = gnext[a * C:(a + 1) * C, :]
        nextg[a, :, Rl:Rl + 128] = val[a * C:(a + 1) * C, :]
        nexth[a] = hnext[a * C:(a + 1) * C, :]
    gn_ref[...] = nextg[c, :, 0:Rl]
    hn_ref[...] = nexth[c]
    lv_ref[...] = nextg[c, :, Rl:Rl + leaves]

    gathered.wait_send()
    for d in list(rows.values()) + list(cods.values()):
        d.wait_send()
    every = grecv.at[pl.ds(1, nc * nr - 1)]
    whole = pltpu.make_async_remote_copy(
        src_ref=every, dst_ref=every, send_sem=g_s, recv_sem=g_r,
        device_id=far_peer(*far[0]), device_id_type=MESH)
    whole.wait_recv()
    top = jnp.max(grecv[...], axis=0)
    for i in range(C):
        line = pltpu.roll(top, (128 - i * nodes) % 128, 1) if i else top
        bg_ref[i:i + 1, :] = line[:, 0:nodes]
    whole.wait_send()


def put(a, b, c, d, oa, ob, oc, od, sems):
    copies = [pltpu.make_async_copy(x, y, sems.at[i])
              for i, (x, y) in enumerate([(a, oa), (b, ob), (c, oc), (d, od)])]
    for x in copies:
        x.start()
    for x in copies:
        x.wait()


def local(codes, split_feature, split_bin, labels, margins):
    Rl, F = codes.shape
    C, NT = split_feature.shape
    nc, nr = lax.axis_size("cls"), lax.axis_size("row")
    nodes = (NT + 1) // 2
    CT, R = C * nc, Rl * nr
    fb = F // (nc * nr)
    chunk = min(4, fb)
    f32, bf16 = jnp.float32, jnp.bfloat16
    pad = -(-NT * C // 16) * 16
    dma = pltpu.SemaphoreType.DMA
    vmem = pl.BlockSpec(memory_space=pltpu.VMEM)
    hbm = pl.BlockSpec(memory_space=pltpu.HBM)
    any_ = pl.BlockSpec(memory_space=pl.ANY)
    shapes = (jax.ShapeDtypeStruct((C, nodes), f32), jax.ShapeDtypeStruct((C, 2 * nodes), f32),
              jax.ShapeDtypeStruct((C, Rl), f32), jax.ShapeDtypeStruct((C, Rl), f32))
    made = pl.pallas_call(
        functools.partial(kernel, (nc, nr, C, Rl, F, NT, chunk)),
        out_shape=shapes,
        in_specs=[hbm] * 5,
        out_specs=(vmem,) * 4,
        scratch_shapes=[
            pltpu.VMEM((Rl, F), jnp.int32), pltpu.VMEM((C, NT), jnp.int32), pltpu.VMEM((C, NT), jnp.int32),
            pltpu.VMEM((1, Rl), jnp.int32), pltpu.VMEM((C, Rl), f32),
            pltpu.VMEM((pad, F), f32), pltpu.VMEM((pad, Rl), f32),
            pltpu.VMEM((nr, fb, Rl), bf16), pltpu.VMEM((nr, fb, Rl), bf16),
            pltpu.VMEM((nc, nr, 2 * C, Rl), f32),
            pltpu.VMEM((CT, R), f32), pltpu.VMEM((CT, R), f32),
            pltpu.VMEM((2 * nodes * CT, R), bf16),
            pltpu.VMEM((fb * BINS, R), bf16),
            pltpu.VMEM((nc, C, Rl + 128), f32), pltpu.VMEM((nc, C, Rl), f32),
            pltpu.VMEM((nc, 1, 128), f32), pltpu.VMEM((nc * nr, 1, 128), f32),
            dma((5,)), dma((nr,)), dma((nr,)), dma(()), dma(()), dma((nr,)), dma((nr,)),
            dma(()), dma(()),
        ],
        compiler_params=pltpu.CompilerParams(
            collective_id=0, has_side_effects=True, vmem_limit_bytes=63 * 2 ** 20),
        name="boost",
    )(codes, split_feature, split_bin, labels.reshape(1, Rl), margins.T)
    best, leaf, grad, hess = pl.pallas_call(
        put, out_shape=shapes, in_specs=[vmem] * 4, out_specs=(any_,) * 4,
        scratch_shapes=[dma((4,))], name="put",
    )(*made)
    return best, leaf, grad.T, hess.T


def solution(mesh):
    in_specs = (P("row", None), P("cls", None), P("cls", None), P("row"), P("row", "cls"))
    out_specs = (P("cls", None), P("cls", None), P("row", "cls"), P("row", "cls"))
    return jax.shard_map(local, mesh=mesh, in_specs=in_specs, out_specs=out_specs, check_vma=False)
```

```python
import functools
import jax
import jax.numpy as jnp
from jax import lax
from jax.experimental import pallas as pl
from jax.experimental.pallas import tpu as pltpu
from jax.sharding import PartitionSpec as P

BINS = 64
REG = 1.0
SHRINK = 0.3
MESH = pl.DeviceIdType.MESH


def kernel(dims, codes_in, sf_in, sb_in, lab_in, mar_in, bg_ref, lv_ref, gn_ref, hn_ref,
           codes_ref, sf_ref, sb_ref, lab_ref, mar_ref, sel, picked, csend, crecv, blocks, marg, tags, wts, le, nextg, nexth,
           gsend, grecv,
           in_s, row_s, row_r, cls_s, cls_r, cod_s, cod_r, g_s, g_r):
    nc, nr, C, Rl, F, NT, chunk = dims
    CT, R = C * nc, Rl * nr
    nodes = (NT + 1) // 2
    leaves = 2 * nodes
    levels = nodes.bit_length() - 1
    fq = F // nc
    fb = fq // nr
    f32, bf16 = jnp.float32, jnp.bfloat16
    c = lax.axis_index("cls")
    r = lax.axis_index("row")

    cls_at = [jnp.where(c + k >= nc, c + k - nc, c + k) for k in range(nc)]
    row_at = [jnp.where(r + k >= nr, r + k - nr, r + k) for k in range(nr)]

    def row_peer(k):
        return (c, row_at[k])

    def cls_peer(k):
        return (cls_at[k], r)

    def far_peer(kc, kr):
        return (cls_at[kc], row_at[kr])

    loads = [pltpu.make_async_copy(src, dst, in_s.at[i]) for i, (src, dst) in enumerate(
        [(sf_in, sf_ref), (codes_in, codes_ref), (sb_in, sb_ref), (lab_in, lab_ref), (mar_in, mar_ref)])]
    for d in loads:
        d.start()
    barrier = pltpu.get_barrier_semaphore()
    far = [(kc, kr) for kc in range(nc) for kr in range(nr) if kc + kr > 0]
    for k in range(1, nr):
        pl.semaphore_signal(barrier, inc=1, device_id=row_peer(k), device_id_type=MESH)
    for k in range(1, nc):
        pl.semaphore_signal(barrier, inc=1, device_id=cls_peer(k), device_id_type=MESH)
    for d in loads:
        d.wait()

    lane = lax.broadcasted_iota(jnp.int32, (C, F), 1)
    sel[...] = jnp.zeros_like(sel)
    for n in range(NT):
        sel[n * C:(n + 1) * C, :] = jnp.where(lane == sf_ref[:, n:n + 1], 1.0, 0.0).astype(f32)
    low = codes_ref[...].astype(f32).astype(bf16)
    picked[...] = lax.dot_general(sel[...].astype(bf16), low, (((1,), (1,)), ((), ())),
                                  preferred_element_type=f32)
    bins = sb_ref[...].astype(f32)
    at = jnp.zeros((C, Rl), jnp.int32)
    for level in range(levels + 1):
        first = 2 ** level - 1
        code = picked[first * C:(first + 1) * C, :]
        cut = jnp.broadcast_to(bins[:, first:first + 1], (C, Rl))
        for j in range(1, 2 ** level):
            n = first + j
            hit = at == j
            code = jnp.where(hit, picked[n * C:(n + 1) * C, :], code)
            cut = jnp.where(hit, bins[:, n:n + 1], cut)
        at = 2 * at + jnp.where(code > cut, 1, 0)
    ids = c * C + lax.broadcasted_iota(jnp.int32, (C, Rl), 0)
    tag = at.astype(f32) + jnp.where(lab_ref[...] == ids, float(leaves), 0.0)
    blocks[c, r, 0:C, :] = mar_ref[...]
    blocks[c, r, C:2 * C, :] = tag

    pl.semaphore_wait(barrier, nr - 1 + nc - 1)

    def row_copy(k):
        return pltpu.make_async_remote_copy(
            src_ref=blocks.at[c, r], dst_ref=blocks.at[c, r], send_sem=row_s.at[k],
            recv_sem=row_r.at[k], device_id=row_peer(k), device_id_type=MESH)

    def cls_copy(k, q):
        return pltpu.make_async_remote_copy(
            src_ref=blocks.at[c, q], dst_ref=blocks.at[c, q], send_sem=cls_s,
            recv_sem=cls_r, device_id=cls_peer(k), device_id_type=MESH)

    def cod_copy(k):
        return pltpu.make_async_remote_copy(
            src_ref=csend.at[row_at[k]], dst_ref=crecv.at[r], send_sem=cod_s.at[k],
            recv_sem=cod_r.at[k], device_id=row_peer(k), device_id_type=MESH)

    near = sorted(range(1, nr), key=lambda k: min(k, nr - k))
    rows = {k: row_copy(k) for k in near}
    for d in rows.values():
        d.start()
    for k in range(1, nc):
        cls_copy(k, r).start()

    quarter = codes_ref[:, pl.ds(pl.multiple_of(c * fq, 128), fq)].astype(f32)
    turned = quarter.T.astype(bf16)
    for j in range(nr):
        csend[j] = turned[j * fb:(j + 1) * fb, :]
    cods = {k: cod_copy(k) for k in near}
    for d in cods.values():
        d.start()
    crecv[r] = csend[r]

    for k in near:
        rows[k].wait_recv()
        for m in range(1, nc):
            cls_copy(m, row_at[(nr - k) % nr]).start()

    group = 16
    steps = [(lax.broadcasted_iota(jnp.int32, (group, Rl), 0) + (g * group + 1)).astype(f32).astype(bf16)
             for g in range(BINS // group)]
    zero, one = jnp.zeros((), bf16), jnp.ones((), bf16)
    for k in [0] + near:
        if k:
            cods[k].wait_recv()
        q = row_at[(nr - k) % nr]
        there = pl.ds(pl.multiple_of(q * Rl, 128), Rl)
        block = crecv[q].astype(f32)
        for f in range(fb):
            row = jnp.broadcast_to(block[f:f + 1, :], (group, Rl)).astype(bf16)
            for g in range(BINS // group):
                base = f * BINS + g * group
                le[base:base + group, there] = jnp.clip(steps[g] - row, zero, one)
    others = blocks.at[pl.ds(0, nc - 1)]
    gathered = pltpu.make_async_remote_copy(
        src_ref=others, dst_ref=others, send_sem=cls_s, recv_sem=cls_r,
        device_id=cls_peer(1), device_id_type=MESH)
    gathered.wait_recv()

    for a in range(nc):
        for q in range(nr):
            marg[a * C:(a + 1) * C, q * Rl:(q + 1) * Rl] = blocks[a, q, 0:C, :]
            tags[a * C:(a + 1) * C, q * Rl:(q + 1) * Rl] = blocks[a, q, C:2 * C, :]

    expon = jnp.exp(marg[...])
    tag_all = tags[...]
    target = jnp.where(tag_all >= leaves, 1.0, 0.0).astype(f32)
    leaf = tag_all - leaves * target
    probab = expon / jnp.sum(expon, axis=0, keepdims=True)
    grad = (probab - target).astype(bf16).astype(f32)
    hess = (2.0 * probab * (1.0 - probab)).astype(bf16).astype(f32)
    g_leaf, h_leaf = [], []
    for n in range(nodes):
        gn_, hn_ = [], []
        for s in range(2):
            hit = leaf == float(2 * n + s)
            gs = jnp.where(hit, grad, 0.0)
            hs = jnp.where(hit, hess, 0.0)
            gn_.append(gs)
            hn_.append(hs)
            g_leaf.append(jnp.sum(gs, axis=1, keepdims=True))
            h_leaf.append(jnp.sum(hs, axis=1, keepdims=True))
        wts[n * CT:(n + 1) * CT, :] = (gn_[0] + gn_[1]).astype(bf16)
        wts[(nodes + n) * CT:(nodes + n + 1) * CT, :] = (hn_[0] + hn_[1]).astype(bf16)
    values = [-SHRINK * g / (h + REG) for g, h in zip(g_leaf, h_leaf)]
    g_all = [g_leaf[2 * n] + g_leaf[2 * n + 1] for n in range(nodes)]
    h_all = [h_leaf[2 * n] + h_leaf[2 * n + 1] for n in range(nodes)]

    width = chunk * BINS
    last = lax.rem(lax.broadcasted_iota(jnp.int32, (CT, width), 1), BINS) == BINS - 1
    best = [None] * nodes
    for i in range(fb // chunk):
        sums = lax.dot_general(wts[...], le[i * width:(i + 1) * width, :], (((1,), (1,)), ((), ())),
                               preferred_element_type=f32)
        for n in range(nodes):
            gl = sums[n * CT:(n + 1) * CT, :]
            hl = sums[(nodes + n) * CT:(nodes + n + 1) * CT, :]
            gr = g_all[n] - gl
            hr = h_all[n] - hl + REG
            hl = hl + REG
            gain = (gl * gl * hr + gr * gr * hl) / (hl * hr)
            gain = jnp.where(last, -jnp.inf, gain)
            best[n] = gain if best[n] is None else jnp.maximum(best[n], gain)

    spot = lax.broadcasted_iota(jnp.int32, (CT, 128), 1)
    place = lax.rem(lax.broadcasted_iota(jnp.int32, (CT, 128), 0), C) * nodes
    tops = jnp.zeros((CT, 128), f32)
    for n in range(nodes):
        top = jnp.max(best[n], axis=1, keepdims=True)
        den = h_all[n] + REG
        top = (top - g_all[n] * g_all[n] / den) / den
        tops = jnp.where(spot == place + n, top, tops)
    for a in range(nc):
        gsend[a] = jnp.sum(tops[a * C:(a + 1) * C, :], axis=0, keepdims=True)

    def g_copy(kc, kr):
        slot = kc * nr + kr
        return pltpu.make_async_remote_copy(
            src_ref=gsend.at[cls_at[kc]], dst_ref=grecv.at[slot], send_sem=g_s,
            recv_sem=g_r, device_id=far_peer(kc, kr), device_id_type=MESH)

    gs_ = [g_copy(kc, kr) for kc, kr in far]
    for d in gs_:
        d.start()
    grecv[0] = gsend[c]

    here = pl.ds(pl.multiple_of(r * Rl, 128), Rl)
    tag_own = tags[:, here]
    target_own = jnp.where(tag_own >= leaves, 1.0, 0.0).astype(f32)
    leaf_own = tag_own - leaves * target_own
    update = jnp.zeros((CT, Rl), f32)
    for l in range(leaves):
        update = jnp.where(leaf_own == float(l), values[l], update)
    expon2 = jnp.exp(marg[:, here] + update)
    prob2 = expon2 / jnp.sum(expon2, axis=0, keepdims=True)
    gnext = prob2 - target_own
    hnext = 2.0 * prob2 * (1.0 - prob2)
    spot2 = lax.broadcasted_iota(jnp.int32, (CT, 128), 1)
    val = jnp.zeros((CT, 128), f32)
    for l in range(leaves):
        val = jnp.where(spot2 == l, values[l], val)
    for a in range(nc):
        nextg[a, :, 0:Rl] = gnext[a * C:(a + 1) * C, :]
        nextg[a, :, Rl:Rl + 128] = val[a * C:(a + 1) * C, :]
        nexth[a] = hnext[a * C:(a + 1) * C, :]
    gn_ref[...] = nextg[c, :, 0:Rl]
    hn_ref[...] = nexth[c]
    lv_ref[...] = nextg[c, :, Rl:Rl + leaves]

    gathered.wait_send()
    for d in list(rows.values()) + list(cods.values()):
        d.wait_send()
    every = grecv.at[pl.ds(1, nc * nr - 1)]
    whole = pltpu.make_async_remote_copy(
        src_ref=every, dst_ref=every, send_sem=g_s, recv_sem=g_r,
        device_id=far_peer(*far[0]), device_id_type=MESH)
    whole.wait_recv()
    top = jnp.max(grecv[...], axis=0)
    for i in range(C):
        line = pltpu.roll(top, (128 - i * nodes) % 128, 1) if i else top
        bg_ref[i:i + 1, :] = line[:, 0:nodes]
    whole.wait_send()


def put(a, b, c, d, oa, ob, oc, od, sems):
    copies = [pltpu.make_async_copy(x, y, sems.at[i])
              for i, (x, y) in enumerate([(a, oa), (b, ob), (c, oc), (d, od)])]
    for x in copies:
        x.start()
    for x in copies:
        x.wait()


def local(codes, split_feature, split_bin, labels, margins):
    Rl, F = codes.shape
    C, NT = split_feature.shape
    nc, nr = lax.axis_size("cls"), lax.axis_size("row")
    nodes = (NT + 1) // 2
    CT, R = C * nc, Rl * nr
    fb = F // (nc * nr)
    chunk = min(4, fb)
    f32, bf16 = jnp.float32, jnp.bfloat16
    pad = -(-NT * C // 16) * 16
    dma = pltpu.SemaphoreType.DMA
    vmem = pl.BlockSpec(memory_space=pltpu.VMEM)
    hbm = pl.BlockSpec(memory_space=pltpu.HBM)
    any_ = pl.BlockSpec(memory_space=pl.ANY)
    shapes = (jax.ShapeDtypeStruct((C, nodes), f32), jax.ShapeDtypeStruct((C, 2 * nodes), f32),
              jax.ShapeDtypeStruct((C, Rl), f32), jax.ShapeDtypeStruct((C, Rl), f32))
    made = pl.pallas_call(
        functools.partial(kernel, (nc, nr, C, Rl, F, NT, chunk)),
        out_shape=shapes,
        in_specs=[hbm] * 5,
        out_specs=(vmem,) * 4,
        scratch_shapes=[
            pltpu.VMEM((Rl, F), jnp.int32), pltpu.VMEM((C, NT), jnp.int32), pltpu.VMEM((C, NT), jnp.int32),
            pltpu.VMEM((1, Rl), jnp.int32), pltpu.VMEM((C, Rl), f32),
            pltpu.VMEM((pad, F), f32), pltpu.VMEM((pad, Rl), f32),
            pltpu.VMEM((nr, fb, Rl), bf16), pltpu.VMEM((nr, fb, Rl), bf16),
            pltpu.VMEM((nc, nr, 2 * C, Rl), f32),
            pltpu.VMEM((CT, R), f32), pltpu.VMEM((CT, R), f32),
            pltpu.VMEM((2 * nodes * CT, R), bf16),
            pltpu.VMEM((fb * BINS, R), bf16),
            pltpu.VMEM((nc, C, Rl + 128), f32), pltpu.VMEM((nc, C, Rl), f32),
            pltpu.VMEM((nc, 1, 128), f32), pltpu.VMEM((nc * nr, 1, 128), f32),
            dma((5,)), dma((nr,)), dma((nr,)), dma(()), dma(()), dma((nr,)), dma((nr,)),
            dma(()), dma(()),
        ],
        compiler_params=pltpu.CompilerParams(
            collective_id=0, has_side_effects=True, vmem_limit_bytes=32 * 2 ** 20),
        name="boost",
    )(*[pltpu.with_memory_space_constraint(x, pltpu.HBM)
        for x in (codes, split_feature, split_bin, labels.reshape(1, Rl), margins.T)])
    best, leaf, grad, hess = pl.pallas_call(
        put, out_shape=shapes, in_specs=[vmem] * 4, out_specs=(hbm,) * 4,
        scratch_shapes=[dma((4,))], name="put",
        compiler_params=pltpu.CompilerParams(vmem_limit_bytes=2 ** 20),
    )(*made)
    return best, leaf, grad.T, hess.T


def solution(mesh):
    in_specs = (P("row", None), P("cls", None), P("cls", None), P("row"), P("row", "cls"))
    out_specs = (P("cls", None), P("cls", None), P("row", "cls"), P("row", "cls"))
    return jax.shard_map(local, mesh=mesh, in_specs=in_specs, out_specs=out_specs, check_vma=False)
```

```python
import functools
import jax
import jax.numpy as jnp
from jax import lax
from jax.experimental import pallas as pl
from jax.experimental.pallas import tpu as pltpu
from jax.sharding import PartitionSpec as P

BINS = 64
REG = 1.0
SHRINK = 0.3
MESH = pl.DeviceIdType.MESH


def kernel(dims, codes_in, sf_in, sb_in, lab_in, mar_in, bg_ref, lv_ref, gn_ref, hn_ref,
           codes_ref, sf_ref, sb_ref, lab_ref, mar_ref, sel, picked, csend, crecv, blocks, marg, tags, wts, le, nextg, nexth,
           gsend, grecv,
           in_s, row_s, row_r, cls_s, cls_r, cod_s, cod_r, g_s, g_r):
    nc, nr, C, Rl, F, NT, chunk = dims
    CT, R = C * nc, Rl * nr
    nodes = (NT + 1) // 2
    leaves = 2 * nodes
    levels = nodes.bit_length() - 1
    fq = F // nc
    fb = fq // nr
    f32, bf16 = jnp.float32, jnp.bfloat16
    c = lax.axis_index("cls")
    r = lax.axis_index("row")

    cls_at = [jnp.where(c + k >= nc, c + k - nc, c + k) for k in range(nc)]
    row_at = [jnp.where(r + k >= nr, r + k - nr, r + k) for k in range(nr)]

    def row_peer(k):
        return (c, row_at[k])

    def cls_peer(k):
        return (cls_at[k], r)

    def far_peer(kc, kr):
        return (cls_at[kc], row_at[kr])

    loads = [pltpu.make_async_copy(src, dst, in_s.at[i]) for i, (src, dst) in enumerate(
        [(sf_in, sf_ref), (codes_in, codes_ref), (sb_in, sb_ref), (lab_in, lab_ref), (mar_in, mar_ref)])]
    for d in loads:
        d.start()
    barrier = pltpu.get_barrier_semaphore()
    far = [(kc, kr) for kc in range(nc) for kr in range(nr) if kc + kr > 0]
    for k in range(1, nr):
        pl.semaphore_signal(barrier, inc=1, device_id=row_peer(k), device_id_type=MESH)
    for k in range(1, nc):
        pl.semaphore_signal(barrier, inc=1, device_id=cls_peer(k), device_id_type=MESH)
    loads[0].wait()

    lane = lax.broadcasted_iota(jnp.int32, (C, F), 1)
    sel[...] = jnp.zeros_like(sel)
    for n in range(NT):
        sel[n * C:(n + 1) * C, :] = jnp.where(lane == sf_ref[:, n:n + 1], 1.0, 0.0).astype(f32)
    for d in loads[1:]:
        d.wait()
    low = codes_ref[...].astype(f32).astype(bf16)
    picked[...] = lax.dot_general(sel[...].astype(bf16), low, (((1,), (1,)), ((), ())),
                                  preferred_element_type=f32)
    bins = sb_ref[...].astype(f32)
    at = jnp.zeros((C, Rl), jnp.int32)
    for level in range(levels + 1):
        first = 2 ** level - 1
        code = picked[first * C:(first + 1) * C, :]
        cut = jnp.broadcast_to(bins[:, first:first + 1], (C, Rl))
        for j in range(1, 2 ** level):
            n = first + j
            hit = at == j
            code = jnp.where(hit, picked[n * C:(n + 1) * C, :], code)
            cut = jnp.where(hit, bins[:, n:n + 1], cut)
        at = 2 * at + jnp.where(code > cut, 1, 0)
    ids = c * C + lax.broadcasted_iota(jnp.int32, (C, Rl), 0)
    tag = at.astype(f32) + jnp.where(lab_ref[...] == ids, float(leaves), 0.0)
    blocks[c, r, 0:C, :] = mar_ref[...]
    blocks[c, r, C:2 * C, :] = tag

    pl.semaphore_wait(barrier, nr - 1 + nc - 1)

    def row_copy(k):
        return pltpu.make_async_remote_copy(
            src_ref=blocks.at[c, r], dst_ref=blocks.at[c, r], send_sem=row_s.at[k],
            recv_sem=row_r.at[k], device_id=row_peer(k), device_id_type=MESH)

    def cls_copy(k, q):
        return pltpu.make_async_remote_copy(
            src_ref=blocks.at[c, q], dst_ref=blocks.at[c, q], send_sem=cls_s,
            recv_sem=cls_r, device_id=cls_peer(k), device_id_type=MESH)

    def cod_copy(k):
        return pltpu.make_async_remote_copy(
            src_ref=csend.at[row_at[k]], dst_ref=crecv.at[r], send_sem=cod_s.at[k],
            recv_sem=cod_r.at[k], device_id=row_peer(k), device_id_type=MESH)

    near = sorted(range(1, nr), key=lambda k: min(k, nr - k))
    rows = {k: row_copy(k) for k in near}
    for d in rows.values():
        d.start()
    for k in range(1, nc):
        cls_copy(k, r).start()

    quarter = codes_ref[:, pl.ds(pl.multiple_of(c * fq, 128), fq)].astype(f32)
    turned = quarter.T.astype(bf16)
    for j in range(nr):
        csend[j] = turned[j * fb:(j + 1) * fb, :]
    cods = {k: cod_copy(k) for k in near}
    for d in cods.values():
        d.start()
    crecv[r] = csend[r]

    for k in near:
        rows[k].wait_recv()
        for m in range(1, nc):
            cls_copy(m, row_at[(nr - k) % nr]).start()

    group = 16
    steps = [(lax.broadcasted_iota(jnp.int32, (group, Rl), 0) + (g * group + 1)).astype(f32).astype(bf16)
             for g in range(BINS // group)]
    zero, one = jnp.zeros((), bf16), jnp.ones((), bf16)
    for k in [0] + near:
        if k:
            cods[k].wait_recv()
        q = row_at[(nr - k) % nr]
        there = pl.ds(pl.multiple_of(q * Rl, 128), Rl)
        block = crecv[q].astype(f32)
        for f in range(fb):
            row = jnp.broadcast_to(block[f:f + 1, :], (group, Rl)).astype(bf16)
            for g in range(BINS // group):
                base = f * BINS + g * group
                le[base:base + group, there] = jnp.clip(steps[g] - row, zero, one)
    others = blocks.at[pl.ds(0, nc - 1)]
    gathered = pltpu.make_async_remote_copy(
        src_ref=others, dst_ref=others, send_sem=cls_s, recv_sem=cls_r,
        device_id=cls_peer(1), device_id_type=MESH)
    gathered.wait_recv()

    for a in range(nc):
        for q in range(nr):
            marg[a * C:(a + 1) * C, q * Rl:(q + 1) * Rl] = blocks[a, q, 0:C, :]
            tags[a * C:(a + 1) * C, q * Rl:(q + 1) * Rl] = blocks[a, q, C:2 * C, :]

    expon = jnp.exp(marg[...])
    tag_all = tags[...]
    target = jnp.where(tag_all >= leaves, 1.0, 0.0).astype(f32)
    leaf = tag_all - leaves * target
    probab = expon / jnp.sum(expon, axis=0, keepdims=True)
    grad = (probab - target).astype(bf16).astype(f32)
    hess = (2.0 * probab * (1.0 - probab)).astype(bf16).astype(f32)
    g_leaf, h_leaf = [], []
    for n in range(nodes):
        gn_, hn_ = [], []
        for s in range(2):
            hit = leaf == float(2 * n + s)
            gs = jnp.where(hit, grad, 0.0)
            hs = jnp.where(hit, hess, 0.0)
            gn_.append(gs)
            hn_.append(hs)
            g_leaf.append(jnp.sum(gs, axis=1, keepdims=True))
            h_leaf.append(jnp.sum(hs, axis=1, keepdims=True))
        wts[n * CT:(n + 1) * CT, :] = (gn_[0] + gn_[1]).astype(bf16)
        wts[(nodes + n) * CT:(nodes + n + 1) * CT, :] = (hn_[0] + hn_[1]).astype(bf16)
    values = [-SHRINK * g / (h + REG) for g, h in zip(g_leaf, h_leaf)]
    g_all = [g_leaf[2 * n] + g_leaf[2 * n + 1] for n in range(nodes)]
    h_all = [h_leaf[2 * n] + h_leaf[2 * n + 1] for n in range(nodes)]

    width = chunk * BINS
    last = lax.rem(lax.broadcasted_iota(jnp.int32, (CT, width), 1), BINS) == BINS - 1
    best = [None] * nodes
    for i in range(fb // chunk):
        sums = lax.dot_general(wts[...], le[i * width:(i + 1) * width, :], (((1,), (1,)), ((), ())),
                               preferred_element_type=f32)
        for n in range(nodes):
            gl = sums[n * CT:(n + 1) * CT, :]
            hl = sums[(nodes + n) * CT:(nodes + n + 1) * CT, :]
            gr = g_all[n] - gl
            hr = h_all[n] - hl + REG
            hl = hl + REG
            gain = (gl * gl * hr + gr * gr * hl) / (hl * hr)
            gain = jnp.where(last, -jnp.inf, gain)
            best[n] = gain if best[n] is None else jnp.maximum(best[n], gain)

    spot = lax.broadcasted_iota(jnp.int32, (CT, 128), 1)
    place = lax.rem(lax.broadcasted_iota(jnp.int32, (CT, 128), 0), C) * nodes
    tops = jnp.zeros((CT, 128), f32)
    for n in range(nodes):
        top = jnp.max(best[n], axis=1, keepdims=True)
        den = h_all[n] + REG
        top = (top - g_all[n] * g_all[n] / den) / den
        tops = jnp.where(spot == place + n, top, tops)
    for a in range(nc):
        gsend[a] = jnp.sum(tops[a * C:(a + 1) * C, :], axis=0, keepdims=True)

    def g_copy(kc, kr):
        slot = kc * nr + kr
        return pltpu.make_async_remote_copy(
            src_ref=gsend.at[cls_at[kc]], dst_ref=grecv.at[slot], send_sem=g_s,
            recv_sem=g_r, device_id=far_peer(kc, kr), device_id_type=MESH)

    gs_ = [g_copy(kc, kr) for kc, kr in sorted(far, key=lambda p: (-min(p[1], nr - p[1]), -p[0]))]
    for d in gs_:
        d.start()
    grecv[0] = gsend[c]

    here = pl.ds(pl.multiple_of(r * Rl, 128), Rl)
    tag_own = tags[:, here]
    target_own = jnp.where(tag_own >= leaves, 1.0, 0.0).astype(f32)
    leaf_own = tag_own - leaves * target_own
    update = jnp.zeros((CT, Rl), f32)
    for l in range(leaves):
        update = jnp.where(leaf_own == float(l), values[l], update)
    expon2 = jnp.exp(marg[:, here] + update)
    prob2 = expon2 / jnp.sum(expon2, axis=0, keepdims=True)
    gnext = prob2 - target_own
    hnext = 2.0 * prob2 * (1.0 - prob2)
    spot2 = lax.broadcasted_iota(jnp.int32, (CT, 128), 1)
    val = jnp.zeros((CT, 128), f32)
    for l in range(leaves):
        val = jnp.where(spot2 == l, values[l], val)
    for a in range(nc):
        nextg[a, :, 0:Rl] = gnext[a * C:(a + 1) * C, :]
        nextg[a, :, Rl:Rl + 128] = val[a * C:(a + 1) * C, :]
        nexth[a] = hnext[a * C:(a + 1) * C, :]
    gn_ref[...] = nextg[c, :, 0:Rl]
    hn_ref[...] = nexth[c]
    lv_ref[...] = nextg[c, :, Rl:Rl + leaves]

    gathered.wait_send()
    for d in list(rows.values()) + list(cods.values()):
        d.wait_send()
    every = grecv.at[pl.ds(1, nc * nr - 1)]
    whole = pltpu.make_async_remote_copy(
        src_ref=every, dst_ref=every, send_sem=g_s, recv_sem=g_r,
        device_id=far_peer(*far[0]), device_id_type=MESH)
    whole.wait_recv()
    top = jnp.max(grecv[...], axis=0)
    for i in range(C):
        line = pltpu.roll(top, (128 - i * nodes) % 128, 1) if i else top
        bg_ref[i:i + 1, :] = line[:, 0:nodes]
    whole.wait_send()


def put(a, b, c, d, oa, ob, oc, od, sems):
    copies = [pltpu.make_async_copy(x, y, sems.at[i])
              for i, (x, y) in enumerate([(a, oa), (b, ob), (c, oc), (d, od)])]
    for x in copies:
        x.start()
    for x in copies:
        x.wait()


def local(codes, split_feature, split_bin, labels, margins):
    Rl, F = codes.shape
    C, NT = split_feature.shape
    nc, nr = lax.axis_size("cls"), lax.axis_size("row")
    nodes = (NT + 1) // 2
    CT, R = C * nc, Rl * nr
    fb = F // (nc * nr)
    chunk = min(8, fb)
    f32, bf16 = jnp.float32, jnp.bfloat16
    pad = -(-NT * C // 16) * 16
    dma = pltpu.SemaphoreType.DMA
    vmem = pl.BlockSpec(memory_space=pltpu.VMEM)
    hbm = pl.BlockSpec(memory_space=pltpu.HBM)
    any_ = pl.BlockSpec(memory_space=pl.ANY)
    shapes = (jax.ShapeDtypeStruct((C, nodes), f32), jax.ShapeDtypeStruct((C, 2 * nodes), f32),
              jax.ShapeDtypeStruct((C, Rl), f32), jax.ShapeDtypeStruct((C, Rl), f32))
    made = pl.pallas_call(
        functools.partial(kernel, (nc, nr, C, Rl, F, NT, chunk)),
        out_shape=shapes,
        in_specs=[hbm] * 5,
        out_specs=(vmem,) * 4,
        scratch_shapes=[
            pltpu.VMEM((Rl, F), jnp.int32), pltpu.VMEM((C, NT), jnp.int32), pltpu.VMEM((C, NT), jnp.int32),
            pltpu.VMEM((1, Rl), jnp.int32), pltpu.VMEM((C, Rl), f32),
            pltpu.VMEM((pad, F), f32), pltpu.VMEM((pad, Rl), f32),
            pltpu.VMEM((nr, fb, Rl), bf16), pltpu.VMEM((nr, fb, Rl), bf16),
            pltpu.VMEM((nc, nr, 2 * C, Rl), f32),
            pltpu.VMEM((CT, R), f32), pltpu.VMEM((CT, R), f32),
            pltpu.VMEM((2 * nodes * CT, R), bf16),
            pltpu.VMEM((fb * BINS, R), bf16),
            pltpu.VMEM((nc, C, Rl + 128), f32), pltpu.VMEM((nc, C, Rl), f32),
            pltpu.VMEM((nc, 1, 128), f32), pltpu.VMEM((nc * nr, 1, 128), f32),
            dma((5,)), dma((nr,)), dma((nr,)), dma(()), dma(()), dma((nr,)), dma((nr,)),
            dma(()), dma(()),
        ],
        compiler_params=pltpu.CompilerParams(
            collective_id=0, has_side_effects=True, vmem_limit_bytes=32 * 2 ** 20),
        name="boost",
    )(*[pltpu.with_memory_space_constraint(x, pltpu.HBM)
        for x in (codes, split_feature, split_bin, labels.reshape(1, Rl), margins.T)])
    best, leaf, grad, hess = pl.pallas_call(
        put, out_shape=shapes, in_specs=[vmem] * 4, out_specs=(hbm,) * 4,
        scratch_shapes=[dma((4,))], name="put",
        compiler_params=pltpu.CompilerParams(vmem_limit_bytes=2 ** 20),
    )(*made)
    return best, leaf, grad.T, hess.T


def solution(mesh):
    in_specs = (P("row", None), P("cls", None), P("cls", None), P("row"), P("row", "cls"))
    out_specs = (P("cls", None), P("cls", None), P("row", "cls"), P("row", "cls"))
    return jax.shard_map(local, mesh=mesh, in_specs=in_specs, out_specs=out_specs, check_vma=False)
```
